512 devices in a mesh: clips: 32 (over y, x, core), slab: 16 (over z).
Axes of the slice: x: 4, y: 4, z: 16, core: 2. Of those that a mesh axis runs over, the one named last changes fastest.
Arguments:
- video: bfloat16 [64, 6, 16, 16, 256], P('clips', None, 'slab'), may hold values from -6 to 6
- clip_blocks: int32 [64], replicated, may hold values from 1 to 3, 128 in all
- deal_order: int32 [32], replicated, may hold values from 0 to 31, each once
- kernel: bfloat16 [256, 3456], P('clips', 'slab'), may hold values from -0.078125 to 0.078125
- gain: float32 [128], replicated, may hold values from 0.25 to 1.75
- bias: float32 [128], replicated, may hold values from -3 to 3
- cotangent: bfloat16 [128, 2, 16, 16, 128], P('clips', None, 'slab'), may hold values from -6 to 6
Outputs:
- activations: bfloat16 [128, 2, 16, 16, 128], P('clips', None, 'slab')
- video_grad: bfloat16 [64, 6, 16, 16, 256], P('clips', None, 'slab')
- kernel_grad: float32 [256, 3456], P('clips', 'slab')
- gain_grad: float32 [128], replicated
- bias_grad: float32 [128], replicated
The draws below stay inside these ranges and needn't reach their ends.
Inputs may be any that keep to these rules, and one draw needn't show every extreme that they name: `clip_blocks`: the blocks of all clips add up to 4 times the number of devices along clips, so every device receives exactly 4 blocks; some clip has 3 blocks. `deal_order`: a permutation of the devices along clips.
All inputs are finite; a program needn't handle non-finite values.
Results may differ from the reference program's by a relative error of at most 0.0049.
Values may be sent and summed in bfloat16 or wider, within the bound.
A program may use at most 64 MiB of HBM per device.

```python
import math
import jax
import jax.numpy as jnp
import numpy as np
from jax import lax

C_IN = 256
C_OUT = 128
GROUPS = 16
TAPS = 27
FB = 2
BMAX = 3
W = 16
CSL = 4
NCLIP = 64
FRAMES = 6
H = 16
N_CLIPS = 32


def level_of(rng, shape, split, least, largest):
    loudness = 1.0
    for dim, parts in split:
        heights = jax.random.uniform(jax.random.fold_in(jax.random.fold_in(rng, 6), dim), (parts,), jnp.float32, least / len(split), largest / len(split))
        loudness = loudness * jnp.repeat(jnp.exp(heights), shape[dim] // parts).reshape((-1,) + (1,) * (len(shape) - 1 - dim))
    return loudness


def length_profile(count, total, most, slope):
    loads = [(1 << 20) // math.isqrt(grade ** slope) + 1 for grade in range(2, count + 1)]
    surplus, given = total - most - (count - 1), [1] * (count - 1)
    while surplus > 0:
        movable = [i for i in range(count - 1) if given[i] < most]
        pool, left = sum([loads[i] for i in movable]), surplus
        for i in movable:
            extra = min(most - given[i], max(1, left * loads[i] // pool), surplus)
            given[i] = given[i] + extra
            surplus = surplus - extra
    return np.array([most] + given)


def ragged(rng, number_of, total, reach, slope):
    if number_of == 2:
        one = jax.random.randint(rng, (), max(1, total - reach), min(reach, total - 1) + 1)
        return jnp.stack([one, total - one])
    sizes = jnp.asarray(length_profile(number_of, total, reach, slope), jnp.int32)
    couples = (number_of - 1) // 2
    donor, sink = sizes[1:1 + 2 * couples:2], sizes[2:2 + 2 * couples:2]
    margin = jnp.minimum(donor - 1, reach - sink)
    moved = jax.random.randint(jax.random.fold_in(rng, 1), (couples,), 0, 1 << 20) % (margin + 1)
    sizes = sizes.at[1:1 + 2 * couples:2].set(donor - moved).at[2:2 + 2 * couples:2].set(sink + moved)
    return sizes[jax.random.permutation(jax.random.fold_in(rng, 2), number_of)]


def normal_values(stream_key, extent, scale, reach, split=(), kind=jnp.bfloat16):
    array = jax.random.normal(stream_key, extent, jnp.float32) * scale
    if len(split) > 0:
        array = level_of(stream_key, extent, split, -0.22, 0.18) * array
    return jnp.clip(array, min=-reach, max=reach).astype(kind)


def setup_inputs(seed: int = 0) -> dict:
    streams_of = jax.random.split(jax.random.key(seed), 8)
    video = normal_values(streams_of[0], (NCLIP, FRAMES, H, W, C_IN), 1.0, 6.0, ((0, 32), (2, 16)))
    clip_blocks = ragged(streams_of[1], NCLIP, CSL * N_CLIPS, BMAX, 2).astype(jnp.int32)
    deal_order = jax.random.permutation(streams_of[2], N_CLIPS).astype(jnp.int32)
    kernel = normal_values(streams_of[3], (C_IN, C_OUT * TAPS), (TAPS * C_IN) ** -0.5, 0.078125, ((0, 32), (1, 16)))
    gain = jnp.clip(1.0 + 0.15 * jax.random.normal(streams_of[4], (C_OUT,), jnp.float32), 0.25, 1.75)
    bias = normal_values(streams_of[5], (C_OUT,), 0.5, 3.0, (), jnp.float32)
    cotangent = normal_values(streams_of[6], (N_CLIPS * CSL, FB, H, W, C_OUT), 1.0, 6.0, ((0, 32), (2, 16)))
    return dict(video=video, clip_blocks=clip_blocks, deal_order=deal_order, kernel=kernel, gain=gain, bias=bias, cotangent=cotangent)


def clip_index(block_id, block_ends):
    return lax.optimization_barrier(jnp.sum((block_ends[None, :] <= block_id[:, None]).astype(jnp.int32), axis=1)).astype(jnp.int32)

def reference(video, clip_blocks, deal_order, kernel, gain, bias, cotangent):
    per_group = C_OUT // GROUPS
    kernel_taps = kernel.reshape(C_IN, C_OUT, TAPS).transpose(2, 0, 1)

    def conv_clip(clip):
        padded = jnp.pad(clip, ((2, 0), (1, 1), (1, 1), (0, 0)))
        totals = jnp.zeros((FRAMES * H * W, C_OUT), jnp.float32)
        for step_a in range(3):
            for step_b in range(3):
                for step_c in range(3):
                    tap_rows = padded[step_a:step_a + FRAMES, step_b:step_b + H, step_c:step_c + W].reshape(-1, C_IN)
                    totals = totals + jnp.dot(tap_rows, kernel_taps[(step_a * 3 + step_b) * 3 + step_c], preferred_element_type=jnp.float32)
        return totals.reshape(FRAMES, H, W, C_OUT)
    conv_out = lax.map(conv_clip, video)
    block_ends = jnp.cumsum(clip_blocks).astype(jnp.int32)
    block_starts = (block_ends - clip_blocks).astype(jnp.int32)
    frame_alive = jnp.arange(FRAMES, dtype=jnp.int32)[None, :] < (clip_blocks * FB)[:, None]
    alive_mask = frame_alive[:, :, None, None, None, None]
    grouped = conv_out.reshape(NCLIP, FRAMES, H, W, GROUPS, per_group)
    counts = (clip_blocks * (FB * H * W * per_group)).astype(jnp.float32)
    sum_first = lax.optimization_barrier(jnp.sum(jnp.where(alive_mask, grouped, 0.0), axis=(1, 2, 3, 5)))
    sum_second = lax.optimization_barrier(jnp.sum(jnp.where(alive_mask, grouped * grouped, 0.0), axis=(1, 2, 3, 5)))
    group_mean = sum_first / counts[:, None]
    group_var = sum_second / counts[:, None] - group_mean * group_mean
    inv_std = lax.rsqrt(group_var + 1e-05)

    def spread(stat):
        return stat[:, None, None, None, :, None]
    normed_groups = (grouped - spread(group_mean)) * spread(inv_std)
    normed = normed_groups.reshape(NCLIP, FRAMES, H, W, C_OUT)
    affine = normed * gain + bias
    act = jax.nn.silu(affine).astype(jnp.bfloat16)
    device_ids = jnp.arange(N_CLIPS, dtype=jnp.int32)
    deal_slot = lax.optimization_barrier(jnp.sum(jnp.where(deal_order[:, None] == device_ids[None, :], device_ids[:, None], 0), axis=0)).astype(jnp.int32)
    row_ids = jnp.arange(N_CLIPS * CSL, dtype=jnp.int32)
    block_id = row_ids % CSL * N_CLIPS + deal_slot[row_ids // CSL]
    clip_of = clip_index(block_id, block_ends)
    block_of = block_id - block_starts[clip_of]
    activations = act.reshape(NCLIP, BMAX, FB, H, W, C_OUT)[clip_of, block_of]
    block_range = jnp.arange(BMAX, dtype=jnp.int32)
    clip_block_id = block_starts[:, None] + block_range[None, :]
    block_alive = block_range[None, :] < clip_blocks[:, None]
    row_of = deal_order[clip_block_id % N_CLIPS] * CSL + clip_block_id // N_CLIPS
    row_of = jnp.where(block_alive, row_of, 0).astype(jnp.int32)
    grad_act = jnp.where(block_alive[:, :, None, None, None, None], cotangent[row_of].astype(jnp.float32), 0.0)
    grad_act = grad_act.reshape(NCLIP, FRAMES, H, W, C_OUT)
    sigmoid = jax.nn.sigmoid(affine)
    grad_affine = grad_act * sigmoid * (1.0 + affine * (1.0 - sigmoid))
    gain_grad = lax.optimization_barrier(jnp.sum(grad_affine * normed, axis=(0, 1, 2, 3)))
    bias_grad = lax.optimization_barrier(jnp.sum(grad_affine, axis=(0, 1, 2, 3)))
    grad_normed = (grad_affine * gain).reshape(NCLIP, FRAMES, H, W, GROUPS, per_group)
    sum_grad = lax.optimization_barrier(jnp.sum(jnp.where(alive_mask, grad_normed, 0.0), axis=(1, 2, 3, 5)))
    sum_cross = lax.optimization_barrier(jnp.sum(jnp.where(alive_mask, grad_normed * normed_groups, 0.0), axis=(1, 2, 3, 5)))
    mean_grad = sum_grad / counts[:, None]
    mean_cross = sum_cross / counts[:, None]
    grad_conv = spread(inv_std) * (grad_normed - spread(mean_grad) - normed_groups * spread(mean_cross))
    grad_conv = jnp.where(alive_mask, grad_conv, 0.0).reshape(NCLIP, FRAMES, H, W, C_OUT).astype(jnp.bfloat16)

    def backward_clip(carry, inputs):
        clip, grad_clip = inputs
        padded = jnp.pad(clip, ((2, 0), (1, 1), (1, 1), (0, 0)))
        grad_padded = jnp.pad(grad_clip, ((0, 2), (1, 1), (1, 1), (0, 0)))
        grad_flat = grad_clip.reshape(-1, C_OUT)
        totals = jnp.zeros((FRAMES * H * W, C_IN), jnp.float32)
        tap_terms = []
        for step_a in range(3):
            for step_b in range(3):
                for step_c in range(3):
                    tap = (step_a * 3 + step_b) * 3 + step_c
                    tap_rows = padded[step_a:step_a + FRAMES, step_b:step_b + H, step_c:step_c + W].reshape(-1, C_IN)
                    tap_terms.append(lax.dot_general(tap_rows, grad_flat, (((0,), (0,)), ((), ())), preferred_element_type=jnp.float32))
                    moved = grad_padded[2 - step_a:2 - step_a + FRAMES, 2 - step_b:2 - step_b + H, 2 - step_c:2 - step_c + W].reshape(-1, C_OUT)
                    totals = totals + lax.dot_general(moved, kernel_taps[tap], (((1,), (1,)), ((), ())), preferred_element_type=jnp.float32)
        return (carry + jnp.stack(tap_terms, axis=0), totals.reshape(FRAMES, H, W, C_IN).astype(jnp.bfloat16))
    kernel_sums, video_grad = lax.scan(backward_clip, jnp.zeros((TAPS, C_IN, C_OUT), jnp.float32), (video, grad_conv))
    kernel_grad = kernel_sums.transpose(1, 2, 0).reshape(C_IN, C_OUT * TAPS)
    return (activations, video_grad, kernel_grad, gain_grad, bias_grad)
```

```python
import functools

import jax
import jax.numpy as jnp
from jax import lax
from jax.experimental import pallas as pl
from jax.experimental.pallas import tpu as pltpu
from jax.sharding import PartitionSpec as P

GROUPS = 16
TAPS = 27
FB = 2
BMAX = 3
MESH = pl.DeviceIdType.MESH


def extended(array, axis, dim):
    size, length = (lax.axis_size(axis), array.shape[dim])
    up = [(i, i + 1) for i in range(size - 1)]
    down = [(j, i) for i, j in up]
    before = lax.ppermute(lax.slice_in_dim(array, length - 1, length, axis=dim), axis, up)
    after = lax.ppermute(lax.slice_in_dim(array, 0, 1, axis=dim), axis, down)
    return jnp.concatenate([before, array, after], axis=dim)


def greet(axis, n, me):
    barrier = pltpu.get_barrier_semaphore()

    def signal(k, carry):
        pl.semaphore_signal(
            barrier, inc=1, device_id={axis: lax.rem(me + k, n)}, device_id_type=MESH
        )
        return carry

    lax.fori_loop(1, n, signal, 0)
    pl.semaphore_wait(barrier, n - 1)


def remote(axis, peer, src, dst, sends, recvs, k):
    return pltpu.make_async_remote_copy(
        src_ref=src,
        dst_ref=dst,
        send_sem=sends.at[k],
        recv_sem=recvs.at[k],
        device_id={axis: peer},
        device_id_type=MESH,
    )


def gather_kernel(axis, n, inner, x_ref, out_ref, sends, recvs, own):
    me = lax.axis_index(axis)
    greet(axis, n, me)
    place = out_ref.at[:, me] if inner else out_ref.at[me]

    def copy(k):
        return remote(axis, lax.rem(me + k, n), x_ref, place, sends, recvs, k)

    def start(k, carry):
        copy(k).start()
        return carry

    def wait(k, carry):
        copy(k).wait()
        return carry

    lax.fori_loop(1, n, start, 0)
    local = pltpu.make_async_copy(x_ref, place, own)
    local.start()
    local.wait()
    lax.fori_loop(1, n, wait, 0)


def gather(x, axis, inner, collective_id):
    n = lax.axis_size(axis)
    shape = (x.shape[0], n) + x.shape[1:] if inner else (n,) + x.shape
    return pl.pallas_call(
        functools.partial(gather_kernel, axis, n, inner),
        out_shape=jax.ShapeDtypeStruct(shape, x.dtype),
        in_specs=[pl.BlockSpec(memory_space=pltpu.VMEM)],
        out_specs=pl.BlockSpec(memory_space=pltpu.VMEM),
        scratch_shapes=[
            pltpu.SemaphoreType.DMA((n,)),
            pltpu.SemaphoreType.DMA((n,)),
            pltpu.SemaphoreType.DMA,
        ],
        compiler_params=pltpu.CompilerParams(collective_id=collective_id, has_side_effects=True),
    )(x)


def reduce_kernel(axis, n, parts, *refs):
    count = len(parts)
    ins, outs = refs[:count], refs[count : 2 * count]
    held, sends, recvs = (refs[2 * count + p * count : 2 * count + (p + 1) * count] for p in range(3))
    own = refs[5 * count]
    me = lax.axis_index(axis)
    greet(axis, n, me)

    def block(p, which):
        if parts[p] is None:
            return ins[p]
        return ins[p].at[which] if parts[p] == 0 else ins[p].at[:, which]

    def copy(p, k):
        peer = lax.rem(me + k, n)
        return remote(axis, peer, block(p, peer), held[p].at[me], sends[p], recvs[p], k)

    def start(k, carry):
        for p in range(count):
            copy(p, k).start()
        return carry

    def wait(k, carry):
        for p in range(count):
            copy(p, k).wait()
        return carry

    lax.fori_loop(1, n, start, 0)
    for p in range(count):
        local = pltpu.make_async_copy(block(p, me), held[p].at[me], own)
        local.start()
        local.wait()
    lax.fori_loop(1, n, wait, 0)
    for p in range(count):
        outs[p][...] = jnp.zeros(outs[p].shape, jnp.float32)

        def add(k, carry):
            outs[p][...] += held[p][k].astype(jnp.float32)
            return carry

        lax.fori_loop(0, n, add, 0)


def reduce(xs, parts, axis, collective_id):
    n = lax.axis_size(axis)
    shapes = []
    for x, part in zip(xs, parts):
        shape = list(x.shape)
        if part is not None:
            del shape[part]
        shapes.append(tuple(shape))
    vmem = pl.BlockSpec(memory_space=pltpu.VMEM)
    count = len(xs)
    return pl.pallas_call(
        functools.partial(reduce_kernel, axis, n, parts),
        out_shape=[jax.ShapeDtypeStruct(shape, jnp.float32) for shape in shapes],
        in_specs=[vmem] * count,
        out_specs=[vmem] * count,
        scratch_shapes=[pltpu.VMEM((n,) + shape, x.dtype) for x, shape in zip(xs, shapes)]
        + [pltpu.SemaphoreType.DMA((n,))] * (2 * count)
        + [pltpu.SemaphoreType.DMA],
        compiler_params=pltpu.CompilerParams(collective_id=collective_id, has_side_effects=True),
    )(*xs)


def picked(mask, array):
    mask = mask.reshape(mask.shape + (1,) * (array.ndim - 1))
    return jnp.sum(jnp.where(mask, array[None], jnp.zeros((), array.dtype)), axis=1)


def nine(padded, columns, flip):
    order = (2, 1, 0) if flip else (0, 1, 2)
    return jnp.concatenate(
        [padded[:, :, b, e : e + columns, :] for b in order for e in order], axis=-1
    )


def body(video, clip_blocks, deal_order, kernel, gain, bias, cotangent):
    clip_devs = lax.axis_size("clips")
    slab_devs = lax.axis_size("slab")
    own_index = lax.axis_index("clips")
    held, frames, row_count, columns, in_channels = video.shape
    slot_count = cotangent.shape[0]
    out_channels = gain.shape[0]
    per_group = out_channels // GROUPS
    capacity = -(-(held * BMAX) // clip_devs)
    highest = lax.Precision.HIGHEST
    block_ends = jnp.cumsum(clip_blocks)
    block_starts = block_ends - clip_blocks
    device_ids = jnp.arange(clip_devs, dtype=jnp.int32)
    deal_slot = jnp.sum(
        jnp.where(deal_order[:, None] == device_ids[None, :], device_ids[:, None], 0), axis=0
    )
    own_slot = jnp.sum(jnp.where(deal_order == own_index, device_ids, 0))
    first_clip = own_index * held
    own_blocks = lax.dynamic_slice(clip_blocks, (first_clip,), (held,))
    own_starts = lax.dynamic_slice(block_starts, (first_clip,), (held,))
    own_start = own_starts[0]
    turn = jnp.arange(capacity, dtype=jnp.int32)

    width = kernel.shape[1]
    lanes = -(-width // 128) * 128
    shards = gather(jnp.pad(kernel, ((0, 0), (0, lanes - width))), "slab", False, 0)
    rows_held = kernel.shape[0]
    own_rows = shards[:, :, :width].transpose(1, 0, 2).reshape(rows_held, out_channels, TAPS)
    taps = gather(own_rows.transpose(2, 0, 1), "clips", True, 1)
    taps = taps.reshape(TAPS, in_channels, out_channels)

    range_start = block_starts.reshape(clip_devs, held)[:, 0]
    range_end = block_ends.reshape(clip_devs, held)[:, held - 1]
    first_block = range_start + jnp.mod(own_slot - range_start, clip_devs)
    block_id = first_block[:, None] + turn[None, :] * clip_devs
    slot_of = jnp.where(block_id < range_end[:, None], block_id // clip_devs, -1).reshape(-1)
    slot_ids = jnp.arange(slot_count, dtype=jnp.int32)
    pieces = picked(slot_of[:, None] == slot_ids[None, :], cotangent)
    returned = lax.all_to_all(
        pieces.reshape((clip_devs, capacity) + pieces.shape[1:]),
        "clips",
        split_axis=0,
        concat_axis=0,
        tiled=True,
    )
    block_range = jnp.arange(BMAX, dtype=jnp.int32)[None, :]
    own_ids = own_starts[:, None] + block_range
    own_live = (block_range < own_blocks[:, None]).reshape(-1)
    source = jnp.sum(
        jnp.where(
            jnp.mod(own_ids, clip_devs).reshape(-1)[:, None] == device_ids[None, :],
            deal_order[None, :],
            0,
        ),
        axis=1,
    )
    came = source * capacity + (own_ids.reshape(-1) - own_start) // clip_devs
    came = jnp.where(own_live, came, -1)
    piece_ids = jnp.arange(clip_devs * capacity, dtype=jnp.int32)
    flat_rows = returned.reshape((clip_devs * capacity,) + returned.shape[2:])
    grad_act = picked(came[:, None] == piece_ids[None, :], flat_rows)
    cells = frames * row_count * columns
    grad_act = grad_act.reshape(held, cells, out_channels).astype(jnp.float32)

    rimmed = extended(video, "slab", 2)
    padded = jnp.pad(rimmed, ((0, 0), (2, 0), (0, 0), (1, 1), (0, 0)))
    side = nine(padded, columns, False)
    weights = taps.reshape(3, 9 * in_channels, out_channels)
    steps = [side[:, a : a + frames].reshape(held * cells, 9 * in_channels) for a in range(3)]
    conv = sum(
        jnp.dot(steps[a], weights[a], preferred_element_type=jnp.float32) for a in range(3)
    ).reshape(held, cells, out_channels)

    cell_frame = jnp.arange(cells, dtype=jnp.int32) // (row_count * columns)
    alive = (cell_frame[None, :] < (own_blocks * FB)[:, None])[:, :, None]
    channel = jnp.arange(out_channels, dtype=jnp.int32) // per_group
    same_group = (channel[:, None] == channel[None, :]).astype(jnp.float32)
    count = (own_blocks * (FB * row_count * slab_devs * columns * per_group)).astype(jnp.float32)
    count = count[:, None]
    live_conv = jnp.where(alive, conv, 0.0)
    rest = jnp.zeros((-(2 * held) % 8, out_channels), jnp.float32)

    def slab_sums(one, two, collective_id):
        packed = jnp.concatenate([one, two, rest], axis=0)
        (sums,) = reduce((packed,), (None,), "slab", collective_id)
        return sums

    def grouped(sums):
        return jnp.dot(sums, same_group, precision=highest)

    sums = grouped(slab_sums(jnp.sum(live_conv, 1), jnp.sum(live_conv * live_conv, 1), 2))
    mean = sums[:held] / count
    variance = sums[held : 2 * held] / count - mean * mean
    inv_std = lax.rsqrt(variance + 1e-05)
    normed = (conv - mean[:, None]) * inv_std[:, None]
    affine = normed * gain + bias
    sigmoid = jax.nn.sigmoid(affine)

    act = jax.nn.silu(affine).astype(jnp.bfloat16)
    act = act.reshape(held * BMAX, FB, row_count, columns, out_channels)
    own_end = own_starts[held - 1] + own_blocks[held - 1]
    first_block = own_start + jnp.mod(deal_slot - own_start, clip_devs)
    block_id = (first_block[:, None] + turn[None, :] * clip_devs).reshape(-1)
    wanted = (block_id[:, None] == own_ids.reshape(-1)[None, :]) & own_live[None, :]
    pieces = picked(wanted & (block_id < own_end)[:, None], act)
    received = lax.all_to_all(
        pieces.reshape((clip_devs, capacity) + pieces.shape[1:]),
        "clips",
        split_axis=0,
        concat_axis=0,
        tiled=True,
    )
    slot_blocks = slot_ids * clip_devs + own_slot
    slot_clip = jnp.sum((block_ends[None, :] <= slot_blocks[:, None]).astype(jnp.int32), axis=1)
    source = slot_clip // held
    source_start = jnp.sum(
        jnp.where(source[:, None] == device_ids[None, :], range_start[None, :], 0), axis=1
    )
    came = source * capacity + (slot_blocks - source_start) // clip_devs
    flat_rows = received.reshape((clip_devs * capacity,) + received.shape[2:])
    activations = picked(came[:, None] == piece_ids[None, :], flat_rows)

    grad_affine = grad_act * sigmoid * (1.0 + affine * (1.0 - sigmoid))
    sums = slab_sums(jnp.sum(grad_affine, 1), jnp.sum(grad_affine * normed, 1), 3)
    means = grouped(sums * gain)
    mean_grad = means[:held] / count
    mean_cross = means[held : 2 * held] / count
    grad_conv = inv_std[:, None] * (
        grad_affine * gain - mean_grad[:, None] - normed * mean_cross[:, None]
    )
    grad_conv = jnp.where(alive, grad_conv, 0.0).astype(jnp.bfloat16)
    bias_own = jnp.sum(sums[:held], axis=0, keepdims=True)
    gain_own = jnp.sum(sums[held : 2 * held], axis=0, keepdims=True)
    small = jnp.concatenate([bias_own, gain_own, jnp.zeros((6, out_channels), jnp.float32)], axis=0)

    grad_flat = grad_conv.reshape(held * cells, out_channels)
    terms = jnp.stack(
        [
            lax.dot_general(
                steps[a],
                grad_flat,
                (((0,), (0,)), ((), ())),
                preferred_element_type=jnp.float32,
            ).astype(jnp.bfloat16)
            for a in range(3)
        ]
    ).reshape(TAPS, clip_devs, rows_held, out_channels)
    rimmed_grad = extended(
        grad_conv.reshape(held, frames, row_count, columns, out_channels), "slab", 2
    )
    own_terms, small_sums = reduce((terms, small), (1, None), "clips", 4)
    own_terms = own_terms.transpose(1, 2, 0).reshape(rows_held, slab_devs, width)
    own_terms = jnp.pad(own_terms.transpose(1, 0, 2), ((0, 0), (0, 0), (0, lanes - width)))
    (kernel_grad,) = reduce((own_terms,), (0,), "slab", 5)

    grad_padded = jnp.pad(rimmed_grad, ((0, 0), (0, 2), (0, 0), (1, 1), (0, 0)))
    grad_side = nine(grad_padded, columns, True)
    turned = taps.reshape(3, 9, in_channels, out_channels).transpose(0, 1, 3, 2)
    turned = turned.reshape(3, 9 * out_channels, in_channels)
    video_grad = sum(
        jnp.dot(
            grad_side[:, 2 - a : 2 - a + frames].reshape(held * cells, 9 * out_channels),
            turned[a],
            preferred_element_type=jnp.float32,
        )
        for a in range(3)
    )
    video_grad = video_grad.reshape(video.shape).astype(jnp.bfloat16)
    return (activations, video_grad, kernel_grad[:, :width], small_sums[1], small_sums[0])


def solution(mesh):
    return jax.shard_map(
        body,
        mesh=mesh,
        in_specs=(
            P("clips", None, "slab", None, None),
            P(),
            P(),
            P("clips", "slab"),
            P(),
            P(),
            P("clips", None, "slab", None, None),
        ),
        out_specs=(
            P("clips", None, "slab", None, None),
            P("clips", None, "slab", None, None),
            P("clips", "slab"),
            P(),
            P(),
        ),
        check_vma=False,
    )
```

```python
import functools

import jax
import jax.numpy as jnp
from jax import lax
from jax.experimental import pallas as pl
from jax.experimental.pallas import tpu as pltpu
from jax.sharding import PartitionSpec as P

GROUPS = 16
TAPS = 27
FB = 2
BMAX = 3
MESH = pl.DeviceIdType.MESH


def extended(array, axis, dim):
    size, length = (lax.axis_size(axis), array.shape[dim])
    up = [(i, i + 1) for i in range(size - 1)]
    down = [(j, i) for i, j in up]
    before = lax.ppermute(lax.slice_in_dim(array, length - 1, length, axis=dim), axis, up)
    after = lax.ppermute(lax.slice_in_dim(array, 0, 1, axis=dim), axis, down)
    return jnp.concatenate([before, array, after], axis=dim)


def greet(axis, n, me):
    barrier = pltpu.get_barrier_semaphore()

    def signal(k, carry):
        pl.semaphore_signal(
            barrier, inc=1, device_id={axis: lax.rem(me + k, n)}, device_id_type=MESH
        )
        return carry

    lax.fori_loop(1, n, signal, 0)
    pl.semaphore_wait(barrier, n - 1)


def remote(axis, peer, src, dst, sends, recvs, k):
    return pltpu.make_async_remote_copy(
        src_ref=src,
        dst_ref=dst,
        send_sem=sends.at[k],
        recv_sem=recvs.at[k],
        device_id={axis: peer},
        device_id_type=MESH,
    )


def gather_kernel(axis, n, inner, x_ref, out_ref, sends, recvs, own):
    me = lax.axis_index(axis)
    greet(axis, n, me)
    place = out_ref.at[:, me] if inner else out_ref.at[me]

    def copy(k):
        return remote(axis, lax.rem(me + k, n), x_ref, place, sends, recvs, k)

    def start(k, carry):
        copy(k).start()
        return carry

    def wait(k, carry):
        copy(k).wait()
        return carry

    lax.fori_loop(1, n, start, 0)
    local = pltpu.make_async_copy(x_ref, place, own)
    local.start()
    local.wait()
    lax.fori_loop(1, n, wait, 0)


def gather(x, axis, inner, collective_id):
    n = lax.axis_size(axis)
    shape = (x.shape[0], n) + x.shape[1:] if inner else (n,) + x.shape
    return pl.pallas_call(
        functools.partial(gather_kernel, axis, n, inner),
        out_shape=jax.ShapeDtypeStruct(shape, x.dtype),
        in_specs=[pl.BlockSpec(memory_space=pltpu.VMEM)],
        out_specs=pl.BlockSpec(memory_space=pltpu.VMEM),
        scratch_shapes=[
            pltpu.SemaphoreType.DMA((n,)),
            pltpu.SemaphoreType.DMA((n,)),
            pltpu.SemaphoreType.DMA,
        ],
        compiler_params=pltpu.CompilerParams(collective_id=collective_id, has_side_effects=True),
    )(x)


def reduce_kernel(axis, n, parts, *refs):
    count = len(parts)
    ins, outs = refs[:count], refs[count : 2 * count]
    held, sends, recvs = (refs[2 * count + p * count : 2 * count + (p + 1) * count] for p in range(3))
    own = refs[5 * count]
    me = lax.axis_index(axis)
    greet(axis, n, me)

    def block(p, which):
        if parts[p] is None:
            return ins[p]
        return ins[p].at[which] if parts[p] == 0 else ins[p].at[:, which]

    def copy(p, k):
        peer = lax.rem(me + k, n)
        return remote(axis, peer, block(p, peer), held[p].at[me], sends[p], recvs[p], k)

    def start(k, carry):
        for p in range(count):
            copy(p, k).start()
        return carry

    def wait(k, carry):
        for p in range(count):
            copy(p, k).wait()
        return carry

    lax.fori_loop(1, n, start, 0)
    for p in range(count):
        local = pltpu.make_async_copy(block(p, me), held[p].at[me], own)
        local.start()
        local.wait()
    lax.fori_loop(1, n, wait, 0)
    for p in range(count):
        outs[p][...] = jnp.zeros(outs[p].shape, jnp.float32)

        def add(k, carry):
            outs[p][...] += held[p][k].astype(jnp.float32)
            return carry

        lax.fori_loop(0, n, add, 0)


def reduce(xs, parts, axis, collective_id):
    n = lax.axis_size(axis)
    shapes = []
    for x, part in zip(xs, parts):
        shape = list(x.shape)
        if part is not None:
            del shape[part]
        shapes.append(tuple(shape))
    vmem = pl.BlockSpec(memory_space=pltpu.VMEM)
    count = len(xs)
    return pl.pallas_call(
        functools.partial(reduce_kernel, axis, n, parts),
        out_shape=[jax.ShapeDtypeStruct(shape, jnp.float32) for shape in shapes],
        in_specs=[vmem] * count,
        out_specs=[vmem] * count,
        scratch_shapes=[pltpu.VMEM((n,) + shape, x.dtype) for x, shape in zip(xs, shapes)]
        + [pltpu.SemaphoreType.DMA((n,))] * (2 * count)
        + [pltpu.SemaphoreType.DMA],
        compiler_params=pltpu.CompilerParams(collective_id=collective_id, has_side_effects=True),
    )(*xs)


def loop(low, high, step):
    def once(k, carry):
        step(k)
        return carry

    lax.fori_loop(low, high, once, 0)


def weights_kernel(n, x_ref, y_ref, out_ref, land_ref, sems, y_sems, own):
    me = lax.axis_index("clips")
    greet("clips", n, me)
    chips = n // 2
    partner = me + 1 - 2 * lax.rem(me, 2)

    def direct(j):
        peer = lax.rem(me + 2 * j, n)
        return remote("clips", peer, x_ref, out_ref.at[:, me], sems.at[0], sems.at[1], j)

    def passed(j):
        place = out_ref.at[:, lax.rem(me + n - 2 * j, n)]
        return remote("clips", partner, place, place, sems.at[2], sems.at[3], j)

    def first():
        return remote("clips", partner, x_ref, out_ref.at[:, me], sems.at[2], sems.at[3], 0)

    def other(k):
        peer = lax.rem(me + k, n)
        return remote(
            "clips", peer, y_ref.at[peer], land_ref.at[me], y_sems.at[0], y_sems.at[1], k
        )

    loop(1, chips, lambda j: direct(j).start())
    first().start()
    loop(1, n, lambda k: other(k).start())
    for source, target in ((x_ref, out_ref.at[:, me]), (y_ref.at[me], land_ref.at[me])):
        local = pltpu.make_async_copy(source, target, own)
        local.start()
        local.wait()

    def relay(j):
        direct(j).wait_recv()
        passed(j).start()

    loop(1, chips, relay)
    loop(1, chips, lambda j: direct(j).wait_send())
    first().wait()
    loop(1, chips, lambda j: passed(j).wait())
    loop(1, n, lambda k: other(k).wait())


def weights_gather(x, y, collective_id):
    n = lax.axis_size("clips")
    vmem = pl.BlockSpec(memory_space=pltpu.VMEM)
    return pl.pallas_call(
        functools.partial(weights_kernel, n),
        out_shape=[
            jax.ShapeDtypeStruct((x.shape[0], n) + x.shape[1:], x.dtype),
            jax.ShapeDtypeStruct(y.shape, y.dtype),
        ],
        in_specs=[vmem] * 2,
        out_specs=[vmem] * 2,
        scratch_shapes=[
            pltpu.SemaphoreType.DMA((4, n // 2)),
            pltpu.SemaphoreType.DMA((2, n)),
            pltpu.SemaphoreType.DMA,
        ],
        compiler_params=pltpu.CompilerParams(collective_id=collective_id, has_side_effects=True),
    )(x, y)


def terms_kernel(
    n, x_ref, s_ref, y_ref, out_ref, sum_ref, land_ref, half, mixed, held, shelf, sems, o_sems, own
):
    me = lax.axis_index("clips")
    greet("clips", n, me)
    chips = n // 2
    core, chip = lax.rem(me, 2), me // 2
    partner = me + 1 - 2 * core

    def near(j):
        c = lax.rem(chip + j, chips)
        return remote(
            "clips", partner, x_ref.at[:, c, 1 - core], half.at[c], sems.at[0], sems.at[1], j
        )

    def far(j):
        c = lax.rem(chip + j, chips)
        return remote(
            "clips", 2 * c + core, mixed.at[c], held.at[chip], sems.at[2], sems.at[3], j
        )

    def summed(k):
        peer = lax.rem(me + k, n)
        return remote("clips", peer, s_ref, shelf.at[me], o_sems.at[0], o_sems.at[1], k)

    def other(k):
        peer = lax.rem(me + k, n)
        return remote(
            "clips", peer, y_ref.at[peer], land_ref.at[me], o_sems.at[2], o_sems.at[3], k
        )

    loop(0, chips, lambda j: near(j).start())

    def mix(j):
        c = lax.rem(chip + j, chips)
        near(j).wait_recv()
        both = x_ref[:, c, core].astype(jnp.float32) + half[c].astype(jnp.float32)
        mixed[c] = both.astype(jnp.bfloat16)
        far(j).start()

    loop(1, chips, mix)
    loop(1, n, lambda k: summed(k).start())
    loop(1, n, lambda k: other(k).start())
    for source, target in ((s_ref, shelf.at[me]), (y_ref.at[me], land_ref.at[me])):
        local = pltpu.make_async_copy(source, target, own)
        local.start()
        local.wait()
    near(0).wait_recv()
    out_ref[...] = x_ref[:, chip, core].astype(jnp.float32) + half[chip].astype(jnp.float32)

    def add(j):
        far(j).wait_recv()
        out_ref[...] += held[lax.rem(chip + chips - j, chips)].astype(jnp.float32)

    loop(1, chips, add)
    loop(0, chips, lambda j: near(j).wait_send())
    loop(1, chips, lambda j: far(j).wait_send())
    loop(1, n, lambda k: summed(k).wait())
    loop(1, n, lambda k: other(k).wait())
    sum_ref[...] = jnp.zeros(sum_ref.shape, jnp.float32)

    def total(k):
        sum_ref[...] += shelf[k]

    loop(0, n, total)


def terms_reduce(x, s, y, collective_id):
    n = lax.axis_size("clips")
    vmem = pl.BlockSpec(memory_space=pltpu.VMEM)
    shape = (x.shape[0],) + x.shape[3:]
    return pl.pallas_call(
        functools.partial(terms_kernel, n),
        out_shape=[
            jax.ShapeDtypeStruct(shape, jnp.float32),
            jax.ShapeDtypeStruct(s.shape, s.dtype),
            jax.ShapeDtypeStruct(y.shape, y.dtype),
        ],
        in_specs=[vmem] * 3,
        out_specs=[vmem] * 3,
        scratch_shapes=[pltpu.VMEM((n // 2,) + shape, x.dtype)] * 3
        + [
            pltpu.VMEM((n,) + s.shape, s.dtype),
            pltpu.SemaphoreType.DMA((4, n // 2)),
            pltpu.SemaphoreType.DMA((4, n)),
            pltpu.SemaphoreType.DMA,
        ],
        compiler_params=pltpu.CompilerParams(collective_id=collective_id, has_side_effects=True),
    )(x, s, y)


def norm_kernel(
    n, clips, conv_ref, grad_ref, alive_ref, count_ref, gain_ref, bias_ref, group_ref,
    act_ref, out_ref, sum_ref, one, two, shelf_one, shelf_two, sems, own,
):
    me = lax.axis_index("slab")
    greet("slab", n, me)

    def total(rows, packed, shelf, base):
        packed[...] = jnp.concatenate(rows, axis=0)

        def copy(k):
            peer = lax.rem(me + k, n)
            return remote("slab", peer, packed, shelf.at[me], sems.at[base], sems.at[base + 1], k)

        loop(1, n, lambda k: copy(k).start())
        local = pltpu.make_async_copy(packed, shelf.at[me], own)
        local.start()
        local.wait()
        loop(1, n, lambda k: copy(k).wait())
        return jnp.sum(shelf[...], axis=0)

    def grouped(sums):
        return jnp.dot(
            sums,
            group_ref[...],
            precision=lax.Precision.HIGHEST,
            preferred_element_type=jnp.float32,
        ) / count_ref[...]

    def rows_of(parts):
        rows = [jnp.sum(part, axis=0, keepdims=True) for part in parts]
        return rows + [jnp.zeros((-len(parts) % 8, gain_ref.shape[1]), jnp.float32)]

    gain, bias = gain_ref[...], bias_ref[...]
    convs = [conv_ref[c] for c in range(clips)]
    lives = [conv_ref[c] * alive_ref[c] for c in range(clips)]
    means = grouped(total(rows_of(lives + [x * x for x in lives]), one, shelf_one, 0))
    normed, grads, inverse = [], [], []
    for c in range(clips):
        mean = means[c : c + 1]
        inv_std = lax.rsqrt(means[clips + c : clips + c + 1] - mean * mean + 1e-05)
        inverse.append(inv_std)
        normed.append((convs[c] - mean) * inv_std)
        affine = normed[c] * gain + bias
        sigmoid = jax.nn.sigmoid(affine)
        act_ref[c] = (affine * sigmoid).astype(act_ref.dtype)
        grads.append(grad_ref[c] * sigmoid * (1.0 + affine * (1.0 - sigmoid)))
    sums = total(
        rows_of(grads + [g * x for g, x in zip(grads, normed)]), two, shelf_two, 2
    )
    sum_ref[...] = sums
    means = grouped(sums * gain)
    for c in range(clips):
        mean, cross = means[c : c + 1], means[clips + c : clips + c + 1]
        grad = inverse[c] * (grads[c] * gain - mean - normed[c] * cross)
        out_ref[c] = (grad * alive_ref[c]).astype(out_ref.dtype)


def normalized(conv, grad, alive, count, gain, bias, group, collective_id):
    n = lax.axis_size("slab")
    vmem = pl.BlockSpec(memory_space=pltpu.VMEM)
    rows = count.shape
    return pl.pallas_call(
        functools.partial(norm_kernel, n, conv.shape[0]),
        out_shape=[
            jax.ShapeDtypeStruct(conv.shape, jnp.bfloat16),
            jax.ShapeDtypeStruct(conv.shape, jnp.bfloat16),
            jax.ShapeDtypeStruct(rows, jnp.float32),
        ],
        in_specs=[vmem] * 7,
        out_specs=[vmem] * 3,
        scratch_shapes=[pltpu.VMEM(rows, jnp.float32)] * 2
        + [pltpu.VMEM((n,) + rows, jnp.float32)] * 2
        + [pltpu.SemaphoreType.DMA((4, n)), pltpu.SemaphoreType.DMA],
        compiler_params=pltpu.CompilerParams(collective_id=collective_id, has_side_effects=True),
    )(conv, grad, alive, count, gain, bias, group)


def picked(mask, array):
    mask = mask.reshape(mask.shape + (1,) * (array.ndim - 1))
    return jnp.sum(jnp.where(mask, array[None], jnp.zeros((), array.dtype)), axis=1)


def nine(padded, columns, flip):
    order = (2, 1, 0) if flip else (0, 1, 2)
    return jnp.concatenate(
        [padded[:, :, b, e : e + columns, :] for b in order for e in order], axis=-1
    )


def body(video, clip_blocks, deal_order, kernel, gain, bias, cotangent):
    clip_devs = lax.axis_size("clips")
    slab_devs = lax.axis_size("slab")
    own_index = lax.axis_index("clips")
    held, frames, row_count, columns, in_channels = video.shape
    slot_count = cotangent.shape[0]
    out_channels = gain.shape[0]
    per_group = out_channels // GROUPS
    capacity = -(-(held * BMAX) // clip_devs)
    block_ends = jnp.cumsum(clip_blocks)
    block_starts = block_ends - clip_blocks
    device_ids = jnp.arange(clip_devs, dtype=jnp.int32)
    deal_slot = jnp.sum(
        jnp.where(deal_order[:, None] == device_ids[None, :], device_ids[:, None], 0), axis=0
    )
    own_slot = jnp.sum(jnp.where(deal_order == own_index, device_ids, 0))
    first_clip = own_index * held
    own_blocks = lax.dynamic_slice(clip_blocks, (first_clip,), (held,))
    own_starts = lax.dynamic_slice(block_starts, (first_clip,), (held,))
    own_start = own_starts[0]
    turn = jnp.arange(capacity, dtype=jnp.int32)

    width = kernel.shape[1]
    lanes = -(-width // 128) * 128
    shards = gather(jnp.pad(kernel, ((0, 0), (0, lanes - width))), "slab", False, 0)
    rows_held = kernel.shape[0]
    own_rows = shards[:, :, :width].transpose(1, 0, 2).reshape(rows_held, out_channels, TAPS)

    range_start = block_starts.reshape(clip_devs, held)[:, 0]
    range_end = block_ends.reshape(clip_devs, held)[:, held - 1]
    first_block = range_start + jnp.mod(own_slot - range_start, clip_devs)
    block_id = first_block[:, None] + turn[None, :] * clip_devs
    slot_of = jnp.where(block_id < range_end[:, None], block_id // clip_devs, -1).reshape(-1)
    slot_ids = jnp.arange(slot_count, dtype=jnp.int32)
    pieces = picked(slot_of[:, None] == slot_ids[None, :], cotangent)
    block_cells = FB * row_count * columns
    pieces = pieces.reshape(clip_devs, capacity * block_cells, out_channels)
    taps, returned = weights_gather(own_rows.transpose(2, 0, 1), pieces, 1)
    taps = taps.reshape(TAPS, in_channels, out_channels)
    block_range = jnp.arange(BMAX, dtype=jnp.int32)[None, :]
    own_ids = own_starts[:, None] + block_range
    own_live = (block_range < own_blocks[:, None]).reshape(-1)
    source = jnp.sum(
        jnp.where(
            jnp.mod(own_ids, clip_devs).reshape(-1)[:, None] == device_ids[None, :],
            deal_order[None, :],
            0,
        ),
        axis=1,
    )
    came = source * capacity + (own_ids.reshape(-1) - own_start) // clip_devs
    came = jnp.where(own_live, came, -1)
    piece_ids = jnp.arange(clip_devs * capacity, dtype=jnp.int32)
    flat_rows = returned.reshape(clip_devs * capacity, block_cells, out_channels)
    grad_act = picked(came[:, None] == piece_ids[None, :], flat_rows)
    cells = frames * row_count * columns
    grad_act = grad_act.reshape(held, cells, out_channels).astype(jnp.float32)

    rimmed = extended(video, "slab", 2)
    padded = jnp.pad(rimmed, ((0, 0), (2, 0), (0, 0), (1, 1), (0, 0)))
    side = nine(padded, columns, False)
    weights = taps.reshape(3, 9 * in_channels, out_channels)
    steps = [side[:, a : a + frames].reshape(held * cells, 9 * in_channels) for a in range(3)]
    conv = sum(
        jnp.dot(steps[a], weights[a], preferred_element_type=jnp.float32) for a in range(3)
    ).reshape(held, cells, out_channels)

    cell_frame = jnp.arange(cells, dtype=jnp.int32) // (row_count * columns)
    alive = (cell_frame[None, :] < (own_blocks * FB)[:, None])[:, :, None]
    channel = jnp.arange(out_channels, dtype=jnp.int32) // per_group
    same_group = (channel[:, None] == channel[None, :]).astype(jnp.float32)
    count = (own_blocks * (FB * row_count * slab_devs * columns * per_group)).astype(jnp.float32)
    padding = jnp.ones((-(2 * held) % 8,), jnp.float32)
    count = jnp.broadcast_to(
        jnp.concatenate([count, count, padding])[:, None], (2 * held + padding.size, out_channels)
    )
    shape = (held, cells, out_channels)
    act, grad_conv, sums = normalized(
        conv,
        grad_act,
        jnp.broadcast_to(alive.astype(jnp.float32), shape),
        count,
        gain[None],
        bias[None],
        same_group,
        2,
    )

    act = act.reshape(held * BMAX, block_cells, out_channels)
    own_end = own_starts[held - 1] + own_blocks[held - 1]
    first_block = own_start + jnp.mod(deal_slot - own_start, clip_devs)
    block_id = (first_block[:, None] + turn[None, :] * clip_devs).reshape(-1)
    wanted = (block_id[:, None] == own_ids.reshape(-1)[None, :]) & own_live[None, :]
    pieces = picked(wanted & (block_id < own_end)[:, None], act)
    act_pieces = pieces.reshape(clip_devs, capacity * block_cells, out_channels)
    slot_blocks = slot_ids * clip_devs + own_slot
    slot_clip = jnp.sum((block_ends[None, :] <= slot_blocks[:, None]).astype(jnp.int32), axis=1)
    source = slot_clip // held
    source_start = jnp.sum(
        jnp.where(source[:, None] == device_ids[None, :], range_start[None, :], 0), axis=1
    )
    came = source * capacity + (slot_blocks - source_start) // clip_devs
    bias_own = jnp.sum(sums[:held], axis=0, keepdims=True)
    gain_own = jnp.sum(sums[held : 2 * held], axis=0, keepdims=True)
    small = jnp.concatenate([bias_own, gain_own, jnp.zeros((6, out_channels), jnp.float32)], axis=0)

    grad_flat = grad_conv.reshape(held * cells, out_channels)
    terms = jnp.stack(
        [
            lax.dot_general(
                steps[a],
                grad_flat,
                (((0,), (0,)), ((), ())),
                preferred_element_type=jnp.float32,
            ).astype(jnp.bfloat16)
            for a in range(3)
        ]
    ).reshape(TAPS, clip_devs // 2, 2, rows_held, out_channels)
    rimmed_grad = extended(
        grad_conv.reshape(held, frames, row_count, columns, out_channels), "slab", 2
    )
    own_terms, small_sums, received = terms_reduce(terms, small, act_pieces, 4)
    flat_rows = received.reshape(clip_devs * capacity, block_cells, out_channels)
    activations = picked(came[:, None] == piece_ids[None, :], flat_rows)
    activations = activations.reshape(cotangent.shape)
    own_terms = own_terms.transpose(1, 2, 0).reshape(rows_held, slab_devs, width)
    own_terms = jnp.pad(own_terms.transpose(1, 0, 2), ((0, 0), (0, 0), (0, lanes - width)))
    (kernel_grad,) = reduce((own_terms,), (0,), "slab", 5)

    grad_padded = jnp.pad(rimmed_grad, ((0, 0), (0, 2), (0, 0), (1, 1), (0, 0)))
    grad_side = nine(grad_padded, columns, True)
    turned = taps.reshape(3, 9, in_channels, out_channels).transpose(0, 1, 3, 2)
    turned = turned.reshape(3, 9 * out_channels, in_channels)
    video_grad = sum(
        jnp.dot(
            grad_side[:, 2 - a : 2 - a + frames].reshape(held * cells, 9 * out_channels),
            turned[a],
            preferred_element_type=jnp.float32,
        )
        for a in range(3)
    )
    video_grad = video_grad.reshape(video.shape).astype(jnp.bfloat16)
    return (activations, video_grad, kernel_grad[:, :width], small_sums[1], small_sums[0])


def solution(mesh):
    return jax.shard_map(
        body,
        mesh=mesh,
        in_specs=(
            P("clips", None, "slab", None, None),
            P(),
            P(),
            P("clips", "slab"),
            P(),
            P(),
            P("clips", None, "slab", None, None),
        ),
        out_specs=(
            P("clips", None, "slab", None, None),
            P("clips", None, "slab", None, None),
            P("clips", "slab"),
            P(),
            P(),
        ),
        check_vma=False,
    )
```
